32 devices in a mesh: dp: 8 (over z, y), tensor: 4 (over x, core).
Axes of the slice: x: 2, y: 2, z: 4, core: 2. Of those that a mesh axis runs over, the one named last changes fastest.
Arguments:
- frames_in: bfloat16 [4096, 1024], P(('dp', 'tensor')), may hold values from -6 to 6
- codes_in: bfloat16 [4096, 3, 1024], P(('dp', 'tensor')), may hold values from -6 to 6
- lengths: int32 [8], P('dp'), may hold values from 64 to 512, as said below
- outer_gain: bfloat16 [1024], replicated, may hold values from 0.099609375 to 1.8984375
- outer_query: bfloat16 [1024, 1024], P(None, 'tensor'), may hold values from -0.1875 to 0.1875
- outer_key: bfloat16 [1024, 1024], P(None, 'tensor'), may hold values from -0.1875 to 0.1875
- outer_value: bfloat16 [1024, 1024], P(None, 'tensor'), may hold values from -0.1875 to 0.1875
- outer_merge: bfloat16 [1024, 1024], P('tensor'), may hold values from -1 to 1
- outer_scale: bfloat16 [1024], replicated, may hold values from 0.099609375 to 1.8984375
- outer_up: bfloat16 [1024, 4096], P(None, 'tensor'), may hold values from -0.1875 to 0.1875
- outer_shift: bfloat16 [4096], P('tensor'), may hold values from -3 to 3
- outer_down: bfloat16 [4096, 1024], P('tensor'), may hold values from -0.09375 to 0.09375
- outer_offset: bfloat16 [1024], replicated, may hold values from -2 to 2
- inner_gain: bfloat16 [1024], replicated, may hold values from 0.099609375 to 1.8984375
- inner_query: bfloat16 [1024, 1024], P(None, 'tensor'), may hold values from -0.1875 to 0.1875
- inner_key: bfloat16 [1024, 1024], P(None, 'tensor'), may hold values from -0.1875 to 0.1875
- inner_value: bfloat16 [1024, 1024], P(None, 'tensor'), may hold values from -0.1875 to 0.1875
- inner_merge: bfloat16 [1024, 1024], P('tensor'), may hold values from -0.25 to 0.25
- inner_scale: bfloat16 [1024], replicated, may hold values from 0.099609375 to 1.8984375
- inner_up: bfloat16 [1024, 4096], P(None, 'tensor'), may hold values from -0.1875 to 0.1875
- inner_shift: bfloat16 [4096], P('tensor'), may hold values from -3 to 3
- inner_down: bfloat16 [4096, 1024], P('tensor'), may hold values from -0.09375 to 0.09375
- inner_offset: bfloat16 [1024], replicated, may hold values from -2 to 2
- cot_global: bfloat16 [4096, 1024], P(('dp', 'tensor')), may hold values from -6 to 6
- cot_local: bfloat16 [4096, 4, 1024], P(('dp', 'tensor')), may hold values from -6 to 6
Outputs:
- global_out: float32 [4096, 1024], P(('dp', 'tensor'))
- local_out: float32 [4096, 4, 1024], P(('dp', 'tensor'))
- grad_frames: float32 [4096, 1024], P(('dp', 'tensor'))
- grad_codes: float32 [4096, 3, 1024], P(('dp', 'tensor'))
- outergain_grad: float32 [1024], replicated
- outerquery_grad: float32 [1024, 1024], P('dp', 'tensor')
- outerkey_grad: float32 [1024, 1024], P('dp', 'tensor')
- outervalue_grad: float32 [1024, 1024], P('dp', 'tensor')
- outermerge_grad: float32 [1024, 1024], P('tensor', 'dp')
- outerscale_grad: float32 [1024], replicated
- outerup_grad: float32 [1024, 4096], P('dp', 'tensor')
- outershift_grad: float32 [4096], replicated
- outerdown_grad: float32 [4096, 1024], P('tensor', 'dp')
- outeroffset_grad: float32 [1024], replicated
- innergain_grad: float32 [1024], replicated
- innerquery_grad: float32 [1024, 1024], P('dp', 'tensor')
- innerkey_grad: float32 [1024, 1024], P('dp', 'tensor')
- innervalue_grad: float32 [1024, 1024], P('dp', 'tensor')
- innermerge_grad: float32 [1024, 1024], P('tensor', 'dp')
- innerscale_grad: float32 [1024], replicated
- innerup_grad: float32 [1024, 4096], P('dp', 'tensor')
- innershift_grad: float32 [4096], replicated
- innerdown_grad: float32 [4096, 1024], P('tensor', 'dp')
- inneroffset_grad: float32 [1024], replicated
The draws below stay inside these ranges and needn't reach their ends.
Inputs may be any that keep to these rules, and one draw needn't show every extreme that they name: Utterance u has its first lengths[u] frames valid and the rest padding; some utterance has exactly 512 valid frames and some exactly 64.
All inputs are finite; a program needn't handle non-finite values.
Results may differ from the reference program's by a relative error of at most 0.02.
Values may be sent and summed in bfloat16 or wider, within the bound.
No kernel may reach another device: no remote copies, remote signals or barrier semaphores. Data moves between devices by JAX's collectives and lax.ppermute only.
A program may use at most 256 MiB of HBM per device.

```python
import jax
import jax.numpy as jnp
from jax import lax

HEADS = 16
HEAD_DIM = 64
D = 1024
FF = 4096
CODEBOOKS = 3
SLOTS = 4
LEN = 512
MIN_LEN = 64
UTTS = 8
FRAMES = 4096


def draw_lengths(key, part):
    first_key = jax.random.fold_in(key, 11)
    second_key = jax.random.fold_in(key, 23)
    counts = jax.random.randint(first_key, (UTTS,), MIN_LEN, LEN + 1)
    shuffled = jax.random.permutation(second_key, UTTS)
    counts = counts.at[shuffled[0]].set(LEN).at[shuffled[1]].set(MIN_LEN)
    return counts.astype(jnp.int32)


def level_of(key, shape, cuts, smallest, largest):
    loudness = 1.0
    for axis_at, blocks in cuts:
        draws = jax.random.uniform(jax.random.fold_in(jax.random.fold_in(key, 6), axis_at), (blocks,), jnp.float32, smallest / len(cuts), largest / len(cuts))
        loudness = loudness * jnp.repeat(jnp.exp(draws), shape[axis_at] // blocks).reshape((-1,) + (1,) * (len(shape) - 1 - axis_at))
    return loudness


def scatter_about(rng, dims, scale, most, pieces=(), kind=jnp.bfloat16):
    level = level_of(rng, dims, pieces, -0.22, 0.18) if pieces else 1.0
    array = jax.random.normal(rng, dims, jnp.float32) * scale * level
    return jnp.minimum(jnp.maximum(array, -most), most).astype(kind)


def setup_inputs(seed: int = 0) -> dict:
    splits = jax.random.split(jax.random.key(seed), 26)
    frames_in = scatter_about(splits[0], (FRAMES, D), 1.0, 6.0, ((0, 32),))
    codes_in = scatter_about(splits[1], (FRAMES, CODEBOOKS, D), 1.0, 6.0, ((0, 32),))
    lengths = draw_lengths(jax.random.fold_in(splits[25], 71), 0)
    outer_gain = jnp.clip(1.0 + 0.18 * jax.random.normal(splits[3], (D,), jnp.float32), 0.099609375, 1.8984375).astype(jnp.bfloat16)
    outer_query = scatter_about(splits[4], (D, D), D ** -0.5, 0.1875, ((1, 4),))
    outer_key = scatter_about(splits[5], (D, D), D ** -0.5, 0.1875, ((1, 4),))
    outer_value = scatter_about(splits[6], (D, D), D ** -0.5, 0.1875, ((1, 4),))
    outer_merge = scatter_about(splits[7], (D, D), (D // 32) ** -0.5, 1.0, ((0, 4),))
    outer_scale = jnp.clip(1.0 + 0.18 * jax.random.normal(splits[8], (D,), jnp.float32), 0.099609375, 1.8984375).astype(jnp.bfloat16)
    outer_up = scatter_about(splits[9], (D, FF), D ** -0.5, 0.1875, ((1, 4),))
    outer_shift = scatter_about(splits[10], (FF,), 0.5, 3.0, ((0, 4),))
    outer_down = scatter_about(splits[11], (FF, D), FF ** -0.5, 0.09375, ((0, 4),))
    outer_offset = scatter_about(splits[12], (D,), 0.3, 2.0)
    inner_gain = jnp.clip(1.0 + 0.18 * jax.random.normal(splits[13], (D,), jnp.float32), 0.099609375, 1.8984375).astype(jnp.bfloat16)
    inner_query = scatter_about(splits[14], (D, D), D ** -0.5, 0.1875, ((1, 4),))
    inner_key = scatter_about(splits[15], (D, D), D ** -0.5, 0.1875, ((1, 4),))
    inner_value = scatter_about(splits[16], (D, D), D ** -0.5, 0.1875, ((1, 4),))
    inner_merge = scatter_about(splits[17], (D, D), (D // 2) ** -0.5, 0.25, ((0, 4),))
    inner_scale = jnp.clip(1.0 + 0.18 * jax.random.normal(splits[18], (D,), jnp.float32), 0.099609375, 1.8984375).astype(jnp.bfloat16)
    inner_up = scatter_about(splits[19], (D, FF), D ** -0.5, 0.1875, ((1, 4),))
    inner_shift = scatter_about(splits[20], (FF,), 0.5, 3.0, ((0, 4),))
    inner_down = scatter_about(splits[21], (FF, D), FF ** -0.5, 0.09375, ((0, 4),))
    inner_offset = scatter_about(splits[22], (D,), 0.3, 2.0)
    cot_global = scatter_about(splits[23], (FRAMES, D), 1.0, 6.0, ((0, 32),))
    cot_local = scatter_about(splits[24], (FRAMES, SLOTS, D), 1.0, 6.0, ((0, 32),))
    return dict(frames_in=frames_in, codes_in=codes_in, lengths=lengths, outer_gain=outer_gain, outer_query=outer_query, outer_key=outer_key, outer_value=outer_value, outer_merge=outer_merge, outer_scale=outer_scale, outer_up=outer_up, outer_shift=outer_shift, outer_down=outer_down, outer_offset=outer_offset, inner_gain=inner_gain, inner_query=inner_query, inner_key=inner_key, inner_value=inner_value, inner_merge=inner_merge, inner_scale=inner_scale, inner_up=inner_up, inner_shift=inner_shift, inner_down=inner_down, inner_offset=inner_offset, cot_global=cot_global, cot_local=cot_local)


@jax.custom_vjp
def low(v):
    return lax.optimization_barrier(v.astype(jnp.bfloat16)).astype(jnp.float32)

@jax.custom_vjp
def low_back(v):
    return v

def low_keep(v):
    return (low(v), None)

def low_pass(kept, grad):
    return (grad,)

def back_keep(v):
    return (v, None)

def back_low(kept, grad):
    return (low(grad),)
low.defvjp(low_keep, low_pass)
low_back.defvjp(back_keep, back_low)
HIGHEST = lax.Precision.HIGHEST
EPSILON = 1e-05
MASKED = -1e+30

def both_round(values):
    return low(low_back(values))

def matmul_high(left, right):
    return jnp.dot(left, right, precision=HIGHEST, preferred_element_type=jnp.float32)

def norm_rows(values, norm_gain):
    return values * lax.rsqrt(lax.optimization_barrier(jnp.mean(values * values, axis=-1, keepdims=True)) + EPSILON) * norm_gain

def global_attend(query_proj, key_proj, value_proj):
    length = query_proj.shape[0]
    block_len = min(512, length)
    score_scale = HEAD_DIM ** (-0.5)
    query_heads = query_proj.reshape(length, HEADS, HEAD_DIM)
    key_heads = key_proj.reshape(length, HEADS, HEAD_DIM)
    value_heads = value_proj.reshape(length, HEADS, HEAD_DIM)
    col_pos = jnp.arange(length).astype(jnp.int32)

    def one_block(row_start):
        block_query = lax.dynamic_slice_in_dim(query_heads, row_start, block_len, 0)
        scores = jnp.einsum('qhd,khd->hqk', block_query, key_heads, precision=HIGHEST) * score_scale
        scores = low_back(scores)
        row_pos = row_start + jnp.arange(block_len).astype(jnp.int32)
        allowed = col_pos[None, None, :] <= row_pos[None, :, None]
        scores = jnp.where(allowed, scores, MASKED)
        attn_probs = low(jax.nn.softmax(scores, axis=-1))
        return jnp.einsum('hqk,khd->qhd', attn_probs, value_heads, precision=HIGHEST)
    starts = (jnp.arange(length // block_len) * block_len).astype(jnp.int32)
    result = lax.map(jax.checkpoint(one_block), starts)
    return result.reshape(length, HEADS * HEAD_DIM)

def local_attend(query_proj, key_proj, value_proj):
    frames = query_proj.shape[0] // SLOTS
    shaped = (frames, SLOTS, HEADS, HEAD_DIM)
    score_scale = HEAD_DIM ** (-0.5)
    scores = jnp.einsum('fqhd,fkhd->fhqk', query_proj.reshape(shaped), key_proj.reshape(shaped), precision=HIGHEST) * score_scale
    scores = low_back(scores)
    allowed = jnp.tril(jnp.ones((SLOTS, SLOTS), jnp.bool_))
    scores = jnp.where(allowed, scores, MASKED)
    attn_probs = low(jax.nn.softmax(scores, axis=-1))
    context = jnp.einsum('fhqk,fkhd->fqhd', attn_probs, value_proj.reshape(shaped), precision=HIGHEST)
    return context.reshape(frames * SLOTS, HEADS * HEAD_DIM)

def block(rows_in, weights, attend):
    gain_attn, w_query, w_key, w_value, w_merge, gain_mlp, w_up, up_bias, w_down, down_bias = weights
    normed = low(norm_rows(rows_in, gain_attn))
    query_proj = both_round(matmul_high(normed, w_query))
    key_proj = both_round(matmul_high(normed, w_key))
    value_proj = both_round(matmul_high(normed, w_value))
    context = both_round(attend(query_proj, key_proj, value_proj))
    middle = rows_in + low_back(matmul_high(context, w_merge))
    normed_mlp = low(norm_rows(middle, gain_mlp))
    hidden_pre = low_back(matmul_high(normed_mlp, w_up) + up_bias)
    hidden_low = low(jax.nn.gelu(hidden_pre))
    return middle + low_back(matmul_high(hidden_low, w_down)) + down_bias

def utterance(outer_params, inner_params, frame_rows, code_rows, valid_rows):
    length = frame_rows.shape[0]
    global_rows = block(frame_rows, outer_params, global_attend)
    sequence = jnp.concatenate([global_rows[:, None, :], code_rows], axis=1).reshape(length * SLOTS, D)
    local_rows = block(sequence, inner_params, local_attend).reshape(length, SLOTS, D)
    return (global_rows * valid_rows[:, None], local_rows * valid_rows[:, None, None])

def reference(frames_in, codes_in, lengths, outer_gain, outer_query, outer_key, outer_value, outer_merge, outer_scale, outer_up, outer_shift, outer_down, outer_offset, inner_gain, inner_query, inner_key, inner_value, inner_merge, inner_scale, inner_up, inner_shift, inner_down, inner_offset, cot_global, cot_local):
    outer = tuple((weight.astype(jnp.float32) for weight in (outer_gain, outer_query, outer_key, outer_value, outer_merge, outer_scale, outer_up, outer_shift, outer_down, outer_offset)))
    inner = tuple((weight.astype(jnp.float32) for weight in (inner_gain, inner_query, inner_key, inner_value, inner_merge, inner_scale, inner_up, inner_shift, inner_down, inner_offset)))
    positions = jnp.arange(LEN).astype(jnp.int32)

    def one_utterance(totals, utter_index):
        row_start = (utter_index * LEN).astype(jnp.int32)
        frame_rows = lax.dynamic_slice_in_dim(frames_in, row_start, LEN, 0).astype(jnp.float32)
        code_rows = lax.dynamic_slice_in_dim(codes_in, row_start, LEN, 0).astype(jnp.float32)
        cot_rows = lax.dynamic_slice_in_dim(cot_global, row_start, LEN, 0).astype(jnp.float32)
        cot_slots = lax.dynamic_slice_in_dim(cot_local, row_start, LEN, 0).astype(jnp.float32)
        valid_rows = (positions < lengths[utter_index]).astype(jnp.float32)

        def forward(outer_params, inner_params, frame_part, code_part):
            return utterance(outer_params, inner_params, frame_part, code_part, valid_rows)
        outputs, pullback = jax.vjp(forward, outer, inner, frame_rows, code_rows)
        grads_outer, grads_inner, grad_frame_rows, grad_code_rows = pullback((cot_rows, cot_slots))
        totals = jax.tree.map(jnp.add, totals, (grads_outer, grads_inner))
        return (totals, (outputs[0], outputs[1], grad_frame_rows, grad_code_rows))
    zero_grads = jax.tree.map(jnp.zeros_like, (outer, inner))
    totals, stacked = lax.scan(one_utterance, zero_grads, jnp.arange(UTTS).astype(jnp.int32))
    global_out = stacked[0].reshape(FRAMES, D)
    local_out = stacked[1].reshape(FRAMES, SLOTS, D)
    grad_frames = stacked[2].reshape(FRAMES, D)
    grad_codes = stacked[3].reshape(FRAMES, CODEBOOKS, D)
    outer_grads, inner_grads = totals
    return (global_out, local_out, grad_frames, grad_codes, outer_grads[0], outer_grads[1], outer_grads[2], outer_grads[3], outer_grads[4], outer_grads[5], outer_grads[6], outer_grads[7], outer_grads[8], outer_grads[9], inner_grads[0], inner_grads[1], inner_grads[2], inner_grads[3], inner_grads[4], inner_grads[5], inner_grads[6], inner_grads[7], inner_grads[8], inner_grads[9])
```

```python
import functools

import jax
import jax.numpy as jnp
from jax import lax
from jax.experimental import pallas as pl
from jax.experimental.pallas import tpu as pltpu
from jax.sharding import PartitionSpec as P

HEAD_DIM = 64
PAIR = 2 * HEAD_DIM
SLOTS = 4
EPSILON = 1e-05
MASKED = -1e30
SCALE = HEAD_DIM ** (-0.5)
F32 = jnp.float32
BF16 = jnp.bfloat16


def norm_rows(values, norm_gain):
    return (
        values * lax.rsqrt(jnp.mean(values * values, axis=-1, keepdims=True) + EPSILON) * norm_gain
    )


def mm(left, right):
    return jnp.dot(left, right, preferred_element_type=F32)


def mm_t(left, right):
    return lax.dot_general(left, right, (((1,), (1,)), ((), ())), preferred_element_type=F32)


def t_mm(left, right):
    return lax.dot_general(left, right, (((0,), (0,)), ((), ())), preferred_element_type=F32)


def swap(values, axis, mask):
    size = lax.axis_size(axis)
    return lax.ppermute(values, axis, [(i, i ^ mask) for i in range(size)])


def bits_of(size):
    return [1 << i for i in range(size.bit_length() - 1)]


def stack_heads(pair):
    lane = lax.broadcasted_iota(jnp.int32, pair.shape, 1)
    low = (lane < HEAD_DIM).astype(F32).astype(BF16)
    high = (lane >= HEAD_DIM).astype(F32).astype(BF16)
    return jnp.concatenate([pair * low, pair * high], axis=0)


def split_heads(stacked):
    rows = stacked.shape[0] // 2
    lane = lax.broadcasted_iota(jnp.int32, (rows, stacked.shape[1]), 1)
    return jnp.where(lane < HEAD_DIM, stacked[:rows], stacked[rows:])


def softmax_of(query2, key, allowed):
    scores = jnp.where(allowed, mm_t(query2, key) * SCALE, MASKED)
    raised = jnp.exp(scores - jnp.max(scores, axis=-1, keepdims=True))
    return raised / jnp.sum(raised, axis=-1, keepdims=True)


def pair_forward(query, key, value, allowed):
    probs = softmax_of(stack_heads(query), key, allowed)
    return split_heads(mm(probs.astype(BF16), value)).astype(BF16)


def pair_backward(query, key, value, grad, allowed):
    query2 = stack_heads(query)
    grad2 = stack_heads(grad)
    probs = softmax_of(query2, key, allowed)
    grad_probs = mm_t(grad2, value)
    row_inner = jnp.sum(probs * grad_probs, axis=-1, keepdims=True)
    grad_scores = (probs * (grad_probs - row_inner)).astype(BF16)
    grad_query = split_heads(mm(grad_scores, key)) * SCALE
    grad_key = t_mm(grad_scores, query2) * SCALE
    grad_value = t_mm(probs.astype(BF16), grad2)
    return grad_query, grad_key, grad_value


def inner_allowed(rows):
    per = rows // SLOTS
    row = lax.broadcasted_iota(jnp.int32, (2 * rows, rows), 0) % rows
    col = lax.broadcasted_iota(jnp.int32, (2 * rows, rows), 1)
    return (row % per == col % per) & (col // per <= row // per)


def inner_forward_kernel(query_ref, key_ref, value_ref, context_ref):
    slots, per, width = query_ref.shape
    rows = slots * per
    allowed = inner_allowed(rows)
    for lane in range(0, width, PAIR):
        pick = lambda ref: ref[:, :, lane : lane + PAIR].reshape(rows, PAIR)
        context = pair_forward(pick(query_ref), pick(key_ref), pick(value_ref), allowed)
        context_ref[:, :, lane : lane + PAIR] = context.reshape(slots, per, PAIR)


def inner_backward_kernel(query_ref, key_ref, value_ref, grad_ref, out_ref):
    slots, per, width = query_ref.shape
    rows = slots * per
    allowed = inner_allowed(rows)
    for lane in range(0, width, PAIR):
        pick = lambda ref: ref[:, :, lane : lane + PAIR].reshape(rows, PAIR)
        grads = pair_backward(
            pick(query_ref), pick(key_ref), pick(value_ref), pick(grad_ref), allowed
        )
        for which, grad in enumerate(grads):
            start = which * width + lane
            out_ref[:, :, start : start + PAIR] = grad.astype(BF16).reshape(slots, per, PAIR)


def inner_specs(frames, width, per):
    piece = lambda which: pl.BlockSpec((SLOTS, per, width), lambda i: (0, i, which))
    return [piece(0), piece(1), piece(2)], (frames // per,)


def inner_attend(projected):
    rows, triple = projected.shape
    frames, width = rows // SLOTS, triple // 3
    per = min(32, frames)
    shaped = projected.reshape(SLOTS, frames, triple)
    specs, grid = inner_specs(frames, width, per)
    context = pl.pallas_call(
        inner_forward_kernel,
        grid=grid,
        in_specs=specs,
        out_specs=pl.BlockSpec((SLOTS, per, width), lambda i: (0, i, 0)),
        out_shape=jax.ShapeDtypeStruct((SLOTS, frames, width), BF16),
        name="inner_attend",
    )(shaped, shaped, shaped)
    return context.reshape(rows, width)


def inner_attend_back(projected, grad_context):
    rows, triple = projected.shape
    frames, width = rows // SLOTS, triple // 3
    per = min(32, frames)
    shaped = projected.reshape(SLOTS, frames, triple)
    specs, grid = inner_specs(frames, width, per)
    grads = pl.pallas_call(
        inner_backward_kernel,
        grid=grid,
        in_specs=specs + [pl.BlockSpec((SLOTS, per, width), lambda i: (0, i, 0))],
        out_specs=pl.BlockSpec((SLOTS, per, triple), lambda i: (0, i, 0)),
        out_shape=jax.ShapeDtypeStruct((SLOTS, frames, triple), BF16),
        name="inner_attend_back",
    )(shaped, shaped, shaped, grad_context.reshape(SLOTS, frames, width))
    return grads.reshape(rows, triple)


def outer_allowed(first, key_pos, rows):
    length = key_pos.shape[1]
    row = lax.broadcasted_iota(jnp.int32, (2 * rows, length), 0) % rows
    return key_pos <= row + first


def outer_forward_kernel(first_ref, key_pos_ref, query_ref, key_ref, value_ref, context_ref):
    allowed = outer_allowed(first_ref[pl.program_id(1)], key_pos_ref[...], query_ref.shape[0])
    context_ref[...] = pair_forward(query_ref[...], key_ref[...], value_ref[...], allowed)


def outer_backward_kernel(
    first_ref,
    key_pos_ref,
    query_ref,
    key_ref,
    value_ref,
    grad_ref,
    grad_query_ref,
    grad_key_ref,
    grad_value_ref,
    key_total,
    value_total,
):
    step = pl.program_id(1)
    allowed = outer_allowed(first_ref[step], key_pos_ref[...], query_ref.shape[0])
    grad_query, grad_key, grad_value = pair_backward(
        query_ref[...], key_ref[...], value_ref[...], grad_ref[...], allowed
    )
    grad_query_ref[...] = grad_query.astype(BF16)

    @pl.when(step == 0)
    def _():
        key_total[...] = grad_key
        value_total[...] = grad_value

    @pl.when(step > 0)
    def _():
        key_total[...] += grad_key
        value_total[...] += grad_value

    @pl.when(step == pl.num_programs(1) - 1)
    def _():
        grad_key_ref[...] = key_total[...].astype(BF16)
        grad_value_ref[...] = value_total[...].astype(BF16)


def outer_attend_specs(length, block, pairs):
    return [
        pl.BlockSpec((1, length), lambda p, i, first: (0, 0)),
        pl.BlockSpec((block, PAIR), lambda p, i, first: (i, p)),
        pl.BlockSpec((length, PAIR), lambda p, i, first: (0, pairs + p)),
        pl.BlockSpec((length, PAIR), lambda p, i, first: (0, 2 * pairs + p)),
    ]


def outer_attend(projected, firsts, key_pos):
    length, triple = projected.shape
    width = triple // 3
    pairs = width // PAIR
    block = length // firsts.shape[0]
    return pl.pallas_call(
        outer_forward_kernel,
        grid_spec=pltpu.PrefetchScalarGridSpec(
            num_scalar_prefetch=1,
            grid=(pairs, length // block),
            in_specs=outer_attend_specs(length, block, pairs),
            out_specs=pl.BlockSpec((block, PAIR), lambda p, i, first: (i, p)),
        ),
        out_shape=jax.ShapeDtypeStruct((length, width), BF16),
        name="outer_attend",
    )(firsts, key_pos, projected, projected, projected)


def outer_attend_back(projected, grad_context, firsts, key_pos):
    length, triple = projected.shape
    width = triple // 3
    pairs = width // PAIR
    block = length // firsts.shape[0]
    by_block = pl.BlockSpec((block, PAIR), lambda p, i, first: (i, p))
    by_pair = pl.BlockSpec((length, PAIR), lambda p, i, first: (0, p))
    whole = jax.ShapeDtypeStruct((length, width), BF16)
    return pl.pallas_call(
        outer_backward_kernel,
        grid_spec=pltpu.PrefetchScalarGridSpec(
            num_scalar_prefetch=1,
            grid=(pairs, length // block),
            in_specs=outer_attend_specs(length, block, pairs) + [by_block],
            out_specs=[by_block, by_pair, by_pair],
            scratch_shapes=[pltpu.VMEM((length, PAIR), F32), pltpu.VMEM((length, PAIR), F32)],
        ),
        out_shape=[whole, whole, whole],
        name="outer_attend_back",
    )(firsts, key_pos, projected, projected, projected, grad_context)


def relative_order():
    size = lax.axis_size("tensor")
    return [k for k in range(size) if not k & 1] + [k for k in range(size) if k & 1]


def gather_rows(values):
    have = {0: values}
    for bit in reversed(bits_of(lax.axis_size("tensor"))):
        have.update({k | bit: swap(v, "tensor", bit) for k, v in list(have.items())})
    return jnp.concatenate([have[k] for k in relative_order()], axis=0)


def reduce_rows(partial_rows):
    order = relative_order()
    rows = partial_rows.shape[0] // len(order)
    have = {k: partial_rows[i * rows : (i + 1) * rows] for i, k in enumerate(order)}
    for bit in bits_of(lax.axis_size("tensor")):
        moved = {
            k: swap(v.astype(BF16), "tensor", bit) for k, v in have.items() if k & bit
        }
        have = {k: v + moved[k | bit].astype(F32) for k, v in have.items() if not k & bit}
    return have[0]


def by_own_bit(first, second, axis, mask):
    mine = (lax.axis_index(axis) & mask) != 0
    return jnp.where(mine, second, first), jnp.where(mine, first, second)


def half_columns(values, axis, mask):
    half = values.shape[1] // 2
    mine = ((lax.axis_index(axis) & mask) != 0).astype(jnp.int32)
    keep = lax.dynamic_slice_in_dim(values, mine * half, half, 1)
    send = lax.dynamic_slice_in_dim(values, (1 - mine) * half, half, 1)
    return keep, send


def order_columns(values, bits):
    count = lax.axis_size("dp")
    block = values.shape[1] // count
    places = []
    for place in range(count):
        index = 0
        for level, bit in enumerate(bits):
            if place >> (len(bits) - 1 - level) & 1:
                index |= bit
        places.append(index)
    return jnp.concatenate([values[:, i * block : (i + 1) * block] for i in places], axis=1)


def scatter_columns(total, bits):
    for bit in bits:
        keep, send = half_columns(total, "dp", bit)
        total = keep + swap(send.astype(BF16), "dp", bit).astype(F32)
    return total


def sum_all(vector):
    for axis in ("dp", "tensor"):
        for bit in bits_of(lax.axis_size(axis)):
            vector = vector + swap(vector, axis, bit)
    return vector


def gather_over_dp(piece):
    rows, width = piece.shape
    have = piece[None]
    for bit in reversed(bits_of(lax.axis_size("dp"))):
        other = swap(have, "dp", bit)
        mine = (lax.axis_index("dp") & bit) != 0
        low = jnp.where(mine, other, have)
        high = jnp.where(mine, have, other)
        have = jnp.stack([low, high], axis=1).reshape(-1, rows, width)
    return have


def gather_weights(shards):
    count = lax.axis_size("dp")
    size = lax.axis_size("tensor")
    here = lax.axis_index("dp")
    cut = [
        lax.dynamic_slice_in_dim(a, here * (a.shape[0] // count), a.shape[0] // count, 0)
        for a in shards
    ]
    groups = {}
    for i, a in enumerate(shards):
        groups.setdefault(a.shape[1], []).append(i)
    have = {0: list(shards)}
    for mask in range(2, size, 2):
        arrays = [None] * len(shards)
        for members in groups.values():
            pack = jnp.concatenate([cut[i] for i in members], axis=0)
            whole = gather_over_dp(swap(pack, "tensor", mask))
            start = 0
            for i in members:
                rows = cut[i].shape[0]
                arrays[i] = whole[:, start : start + rows].reshape(shards[i].shape)
                start += rows
        have[mask] = arrays
    for mask in range(0, size, 2):
        have[mask | 1] = [swap(a, "tensor", 1) for a in have[mask]]
    return have


def outer_forward(rows_in, weights, firsts, key_pos):
    gain_attn, w_qkv, w_merge, gain_mlp, w_up, up_bias, w_down, down_bias = weights
    gathered = gather_rows(norm_rows(rows_in, gain_attn).astype(BF16))
    projected = mm(gathered, w_qkv).astype(BF16)
    context = outer_attend(projected, firsts, key_pos)
    middle = rows_in + reduce_rows(mm(context, w_merge))
    gathered_mlp = gather_rows(norm_rows(middle, gain_mlp).astype(BF16))
    hidden_pre = mm(gathered_mlp, w_up) + up_bias
    hidden_low = jax.nn.gelu(hidden_pre).astype(BF16)
    output = middle + reduce_rows(mm(hidden_low, w_down)) + down_bias
    stored = (rows_in, middle, gathered, projected, context, gathered_mlp, hidden_pre, hidden_low)
    return output, stored


def outer_backward(grad_output, weights, stored, firsts, key_pos):
    gain_attn, w_qkv, w_merge, gain_mlp, w_up, up_bias, w_down, down_bias = weights
    rows_in, middle, gathered, projected, context, gathered_mlp, hidden_pre, hidden_low = stored
    bits = bits_of(lax.axis_size("dp"))
    grad_offset = jnp.sum(grad_output, axis=0)
    grad_full = gather_rows(grad_output.astype(BF16))
    grad_hidden = mm_t(grad_full, w_down)
    grad_pre = jax.vjp(jax.nn.gelu, hidden_pre)[1](grad_hidden)[0].astype(BF16)
    grad_down = scatter_columns(t_mm(hidden_low, order_columns(grad_full, bits)), bits)
    grad_shift = jnp.sum(grad_pre, axis=0, dtype=F32)
    grad_up = scatter_columns(t_mm(grad_pre, order_columns(gathered_mlp, bits)), bits)
    grad_normed_mlp = reduce_rows(mm_t(grad_pre, w_up))
    grad_middle_norm, grad_scale = jax.vjp(norm_rows, middle, gain_mlp)[1](grad_normed_mlp)
    grad_middle = grad_output + grad_middle_norm
    grad_branch = gather_rows(grad_middle.astype(BF16))
    grad_merge = scatter_columns(t_mm(context, order_columns(grad_branch, bits)), bits)
    grad_context = mm_t(grad_branch, w_merge).astype(BF16)
    grad_joined = jnp.concatenate(
        outer_attend_back(projected, grad_context, firsts, key_pos), axis=1
    )
    grad_qkv = scatter_columns(t_mm(grad_joined, order_columns(gathered, bits)), bits)
    grad_normed = reduce_rows(mm_t(grad_joined, w_qkv))
    grad_rows_norm, grad_gain = jax.vjp(norm_rows, rows_in, gain_attn)[1](grad_normed)
    grads = (grad_gain, grad_qkv, grad_merge, grad_scale, grad_up, grad_shift, grad_down, grad_offset)
    return grad_middle + grad_rows_norm, grads


def scatter_shards(own, send, bits):
    del send
    have = own
    for bit in bits_of(lax.axis_size("tensor")):
        moved = {k: swap(v.astype(BF16), "tensor", bit) for k, v in have.items() if k & bit}
        have = {k: v + moved[k | bit].astype(F32) for k, v in have.items() if not k & bit}
    return scatter_columns(have[0], bits)


def inner_block(sequence, grad_rows, small, full):
    gain_attn, gain_mlp, up_bias, down_bias = small
    keys = sorted(full)
    bits = bits_of(lax.axis_size("dp"))
    width = full[0][1].shape[0]
    w_qkv = jnp.concatenate(
        [full[k][0][:, i * width : (i + 1) * width] for i in range(3) for k in keys], axis=1
    )
    w_merge = jnp.concatenate([full[k][1] for k in keys], axis=0)
    normed = norm_rows(sequence, gain_attn).astype(BF16)
    projected = mm(normed, w_qkv).astype(BF16)
    context = inner_attend(projected)
    middle = sequence + mm(context, w_merge)
    normed_mlp = norm_rows(middle, gain_mlp).astype(BF16)
    hidden_pre = {k: mm(normed_mlp, full[k][2]) + up_bias[k] for k in keys}
    hidden_low = {k: jax.nn.gelu(v).astype(BF16) for k, v in hidden_pre.items()}
    output = middle + sum(mm(hidden_low[k], full[k][3]) for k in keys) + down_bias

    grad_offset = jnp.sum(grad_rows, axis=0)
    grad_low = grad_rows.astype(BF16)
    ordered = order_columns(grad_low, bits)
    grad_down = scatter_shards({k: t_mm(hidden_low[k], ordered) for k in keys}, None, bits)
    grad_hidden = {k: mm_t(grad_low, full[k][3]) for k in keys}
    grad_pre = {
        k: jax.vjp(jax.nn.gelu, hidden_pre[k])[1](grad_hidden[k])[0].astype(BF16) for k in keys
    }
    grad_shift = {k: jnp.sum(grad_pre[k], axis=0, dtype=F32) for k in keys}
    ordered = order_columns(normed_mlp, bits)
    grad_up = scatter_shards({k: t_mm(grad_pre[k], ordered) for k in keys}, None, bits)
    grad_normed_mlp = sum(mm_t(grad_pre[k], full[k][2]) for k in keys)
    grad_middle_norm, grad_scale = jax.vjp(norm_rows, middle, gain_mlp)[1](grad_normed_mlp)
    grad_middle = grad_rows + grad_middle_norm
    grad_branch = grad_middle.astype(BF16)
    ordered = order_columns(grad_branch, bits)
    grad_merge = scatter_shards(
        {k: t_mm(context[:, i * width : (i + 1) * width], ordered) for i, k in enumerate(keys)},
        None,
        bits,
    )
    grad_context = mm_t(grad_branch, w_merge).astype(BF16)
    grad_joined = inner_attend_back(projected, grad_context)
    ordered = order_columns(normed, bits)
    whole = width * len(keys)

    def joined_of(i):
        return jnp.concatenate(
            [grad_joined[:, j * whole + i * width : j * whole + (i + 1) * width] for j in range(3)],
            axis=1,
        )

    grad_qkv = scatter_shards(
        {k: t_mm(joined_of(i), ordered) for i, k in enumerate(keys)}, None, bits
    )
    grad_normed = mm_t(grad_joined, w_qkv)
    grad_rows_norm, grad_gain = jax.vjp(norm_rows, sequence, gain_attn)[1](grad_normed)
    grads = (grad_gain, grad_qkv, grad_merge, grad_scale, grad_up, grad_shift, grad_down, grad_offset)
    return output, grad_middle + grad_rows_norm, grads


def place_columns(values, total, which):
    return lax.dynamic_update_slice(
        jnp.zeros((total,), F32), values, (which * values.shape[0],)
    )


def matrix_outputs(grads):
    grad_gain, grad_qkv, grad_merge, grad_scale, grad_up, grad_shift, grad_down, grad_offset = grads
    width = grad_qkv.shape[0] // 3
    turned = grad_qkv.T
    return (
        turned[:, :width],
        turned[:, width : 2 * width],
        turned[:, 2 * width :],
        grad_merge,
        grad_up.T,
        grad_down,
    )


def per_device(
    frames_in,
    codes_in,
    lengths,
    outer_gain,
    outer_query,
    outer_key,
    outer_value,
    outer_merge,
    outer_scale,
    outer_up,
    outer_shift,
    outer_down,
    outer_offset,
    inner_gain,
    inner_query,
    inner_key,
    inner_value,
    inner_merge,
    inner_scale,
    inner_up,
    inner_shift,
    inner_down,
    inner_offset,
    cot_global,
    cot_local,
):
    rows, dim = frames_in.shape
    size = lax.axis_size("tensor")
    here = lax.axis_index("tensor")
    hidden = inner_up.shape[1]
    order = relative_order()
    firsts = jnp.stack([(here ^ k) * rows for k in order]).astype(jnp.int32)
    key_pos = (firsts[:, None] + jnp.arange(rows, dtype=jnp.int32)[None, :]).reshape(1, -1)
    positions = here * rows + jnp.arange(rows, dtype=jnp.int32)
    valid_rows = (positions < lengths[0]).astype(F32)

    full = gather_weights(
        [
            jnp.concatenate([inner_query, inner_key, inner_value], axis=1),
            inner_merge,
            inner_up,
            inner_down,
        ]
    )
    all_shift = lax.all_gather(inner_shift, "tensor", axis=0, tiled=False)
    shift_of = {
        k: lax.dynamic_index_in_dim(all_shift, here ^ k, 0, keepdims=False).astype(F32)
        for k in range(size)
    }

    outer_weights = (
        outer_gain.astype(F32),
        jnp.concatenate([outer_query, outer_key, outer_value], axis=1),
        outer_merge,
        outer_scale.astype(F32),
        outer_up,
        outer_shift.astype(F32),
        outer_down,
        outer_offset.astype(F32),
    )
    global_rows, outer_stored = outer_forward(
        frames_in.astype(F32), outer_weights, firsts, key_pos
    )
    sequence = jnp.concatenate(
        [global_rows[None], jnp.transpose(codes_in, (1, 0, 2)).astype(F32)], axis=0
    ).reshape(SLOTS * rows, dim)
    grad_local = (
        jnp.transpose(cot_local, (1, 0, 2)).astype(F32) * valid_rows[None, :, None]
    ).reshape(SLOTS * rows, dim)
    small = (
        inner_gain.astype(F32),
        inner_scale.astype(F32),
        shift_of,
        inner_offset.astype(F32),
    )
    local_rows, grad_sequence, inner_grads = inner_block(sequence, grad_local, small, full)
    grad_sequence = grad_sequence.reshape(SLOTS, rows, dim)
    grad_global = cot_global.astype(F32) * valid_rows[:, None] + grad_sequence[0]
    grad_frames, outer_grads = outer_backward(
        grad_global, outer_weights, outer_stored, firsts, key_pos
    )
    inner_shift_full = jnp.zeros((size, hidden), F32)
    for k in range(size):
        inner_shift_full = lax.dynamic_update_slice(
            inner_shift_full, inner_grads[5][k][None], (here ^ k, 0)
        )
    pieces = [
        outer_grads[0],
        outer_grads[3],
        outer_grads[7],
        place_columns(outer_grads[5], hidden * size, here),
        inner_grads[0],
        inner_grads[3],
        inner_grads[7],
        inner_shift_full.reshape(-1),
    ]
    summed = sum_all(jnp.concatenate(pieces).reshape(-1, 128)).reshape(-1)
    vectors = []
    start = 0
    for piece in pieces:
        vectors.append(summed[start : start + piece.shape[0]])
        start += piece.shape[0]
    outer_mats = matrix_outputs(outer_grads)
    inner_mats = matrix_outputs(inner_grads)
    local_out = jnp.transpose(local_rows.reshape(SLOTS, rows, dim), (1, 0, 2))
    return (
        global_rows * valid_rows[:, None],
        local_out * valid_rows[:, None, None],
        grad_frames,
        jnp.transpose(grad_sequence[1:], (1, 0, 2)),
        vectors[0],
        *outer_mats[:4],
        vectors[1],
        outer_mats[4],
        vectors[3],
        outer_mats[5],
        vectors[2],
        vectors[4],
        *inner_mats[:4],
        vectors[5],
        inner_mats[4],
        vectors[7],
        inner_mats[5],
        vectors[6],
    )


def solution(mesh):
    in_specs = (
        P(("dp", "tensor"), None),
        P(("dp", "tensor"), None, None),
        P("dp"),
        P(),
        P(None, "tensor"),
        P(None, "tensor"),
        P(None, "tensor"),
        P("tensor", None),
        P(),
        P(None, "tensor"),
        P("tensor"),
        P("tensor", None),
        P(),
        P(),
        P(None, "tensor"),
        P(None, "tensor"),
        P(None, "tensor"),
        P("tensor", None),
        P(),
        P(None, "tensor"),
        P("tensor"),
        P("tensor", None),
        P(),
        P(("dp", "tensor"), None),
        P(("dp", "tensor"), None, None),
    )
    out_specs = (
        P(("dp", "tensor"), None),
        P(("dp", "tensor"), None, None),
        P(("dp", "tensor"), None),
        P(("dp", "tensor"), None, None),
        P(),
        P("dp", "tensor"),
        P("dp", "tensor"),
        P("dp", "tensor"),
        P("tensor", "dp"),
        P(),
        P("dp", "tensor"),
        P(),
        P("tensor", "dp"),
        P(),
        P(),
        P("dp", "tensor"),
        P("dp", "tensor"),
        P("dp", "tensor"),
        P("tensor", "dp"),
        P(),
        P("dp", "tensor"),
        P(),
        P("tensor", "dp"),
        P(),
    )
    return jax.shard_map(
        per_device, mesh=mesh, in_specs=in_specs, out_specs=out_specs, check_vma=False
    )
```
